256 devices in a mesh: row: 16 (over y, x), col: 8 (over z), layer: 2 (over core).
Axes of the slice: x: 4, y: 4, z: 8, core: 2. Of those that a mesh axis runs over, the one named last changes fastest.
Arguments:
- density: bfloat16 [4096, 4096], P('row', ('col', 'layer')), as said below
- cotangent: bfloat16 [4096, 4096], P('row', ('col', 'layer')), may hold values from -6 to 6
- block_pattern: int32 [2, 362], replicated, may hold values from 0 to 31, as said below
Outputs:
- gradient: float32 [4096, 4096], P('row', ('col', 'layer'))
The draws below stay inside these ranges and needn't reach their ends.
Inputs may be any that keep to these rules, and one draw needn't show every extreme that they name: `block_pattern`: each column names one nonzero block; no block is named twice; every block (c, r) is listed with (r, c); all 32 diagonal blocks are listed, and 165 blocks above the diagonal. density is symmetric.
All inputs are finite; a program needn't handle non-finite values.
Results may differ from the reference program's by a relative error of at most 0.0025.
Values may be sent and summed in bfloat16 or wider, within the bound.
No kernel may reach another device: no remote copies, remote signals or barrier semaphores. Data moves between devices by JAX's collectives and lax.ppermute only.
A program may use at most 64 MiB of HBM per device.

```python
import jax
import jax.numpy as jnp
import numpy as np

BS = 128
NB = 32
NN = 4096
OFF = 165


def draw_block_pattern(key, part):
    upper_a, upper_b = np.triu_indices(NB, 1)
    table_a = jnp.asarray(upper_a.astype(np.int32))
    table_b = jnp.asarray(upper_b.astype(np.int32))
    chosen = jax.random.permutation(jax.random.fold_in(key, 11), NB * (NB - 1) // 2)[:OFF]
    first = table_a[chosen]
    second = table_b[chosen]
    diagonal = jnp.arange(NB, dtype=jnp.int32)
    rows_list = jnp.concatenate([diagonal, first, second])
    cols_list = jnp.concatenate([diagonal, second, first])
    return jnp.stack([rows_list, cols_list]).astype(jnp.int32)


def draw_density(key, part):
    sigma = (NB * BS / 3.0) ** (-0.5)
    noise = jax.random.normal(jax.random.fold_in(key, 5), (NB * BS, NB * BS), jnp.float32)
    both = (noise + noise.T) * 0.5 ** 0.5 * sigma
    return both.astype(jnp.bfloat16)


def steps_of(stream_key, extent, pieces, least, top_value):
    def one(position, blocks):
        draws = jax.random.uniform(jax.random.fold_in(jax.random.fold_in(stream_key, 6), position), (blocks,), jnp.float32, least / len(pieces), top_value / len(pieces))
        return jnp.repeat(jnp.exp(draws), extent[position] // blocks).reshape((-1,) + (1,) * (len(extent) - position - 1))

    gain = one(*pieces[0])
    for cut in pieces[1:]:
        gain = gain * one(*cut)
    return gain


def centred(key, extent, spread, bound, split=(), held_as=jnp.bfloat16):
    drawn = spread * jax.random.normal(key, extent, jnp.float32)
    if split:
        drawn = drawn * steps_of(key, extent, split, -0.22, 0.18)
    return jnp.clip(drawn, -bound, bound).astype(held_as)


def setup_inputs(seed: int = 0) -> dict:
    keys = jax.random.split(jax.random.key(seed), 4)
    density = draw_density(jax.random.fold_in(keys[3], 71), 0)
    cotangent = centred(keys[1], (NN, NN), 1.0, 6.0, ((0, 16), (1, 16)))
    block_pattern = draw_block_pattern(jax.random.fold_in(keys[3], 71), 0)
    return {"density": density, "cotangent": cotangent, "block_pattern": block_pattern}


def reference(density, cotangent, block_pattern):
    blocks = jnp.zeros((NB, NB), jnp.float32).at[block_pattern[0], block_pattern[1]].set(1.0)
    mask = jnp.repeat(jnp.repeat(blocks, BS, axis=0), BS, axis=1) > 0.5
    xm = jnp.where(mask, density, jnp.zeros_like(density))
    square = jnp.where(mask, jnp.dot(xm, xm, preferred_element_type=jnp.float32), 0.0).astype(jnp.bfloat16)
    masked_grad = jnp.where(mask, cotangent, jnp.zeros_like(cotangent))
    grad_times = jnp.dot(masked_grad, xm, preferred_element_type=jnp.float32)
    pulled = jnp.where(mask, 3.0 * masked_grad.astype(jnp.float32) - 2.0 * grad_times, 0.0).astype(jnp.bfloat16)
    first_term = jnp.dot(square, masked_grad, preferred_element_type=jnp.float32)
    second_term = jnp.dot(pulled, xm, preferred_element_type=jnp.float32)
    third_term = jnp.dot(xm, pulled, preferred_element_type=jnp.float32)
    return jnp.where(mask, -2.0 * first_term + second_term + third_term, 0.0)
```

```python
import jax
import jax.numpy as jnp
from jax import lax
from jax.experimental import pallas as pl
from jax.experimental.pallas import tpu as pltpu
from jax.sharding import PartitionSpec as P

BS = 128
T = 256
NK = 16
NX = NY = 4
NZ = 8
RING4 = (0, -1, 1, -2)


VMEM = pl.BlockSpec(memory_space=pltpu.VMEM)
BF16 = jnp.bfloat16
F32 = jnp.float32


def shift_x(value, by):
    perm = [(y * NX + x, y * NX + (x + by) % NX) for y in range(NY) for x in range(NX)]
    return lax.ppermute(value, "row", perm)


def shift_y(value, by):
    perm = [(y * NX + x, ((y + by) % NY) * NX + x) for y in range(NY) for x in range(NX)]
    return lax.ppermute(value, "row", perm)


def swap(value):
    return lax.ppermute(value, "layer", [(0, 1), (1, 0)])


def shift_z(value):
    perm = [(z * 2, (z + 1) % NZ * 2) for z in range(NZ)]
    perm += [(z * 2 + 1, (z - 1) % NZ * 2 + 1) for z in range(NZ)]
    return lax.ppermute(value, ("col", "layer"), perm)


def gather_z(own):
    sib = swap(own)
    pair = jnp.concatenate([own, sib], 0)
    got = [shift_z(pair)]
    got.append(shift_z(got[0]))
    got.append(shift_z(got[1]))
    far = shift_z(got[2][: own.shape[0]])
    other = [swap(g) for g in got]
    return [own, sib, *got, *other, far, swap(far)]


def row_pieces(refs, z, layer, height, at, rows):
    own, sib, g1, g2, g3, o1, o2, o3, far, sfar = refs
    s = 2 * layer - 1

    def k_of(dz, lay):
        return lax.rem(z + dz + 2 * NZ, NZ) * 2 + lay

    out = [(k_of(0, layer), own, at), (k_of(0, 1 - layer), sib, at)]
    for j, ref in enumerate((g1, g2, g3), 1):
        out += [(k_of(s * j, layer), ref, at), (k_of(s * j, 1 - layer), ref, height + at)]
    for j, ref in enumerate((o1, o2, o3), 1):
        out += [(k_of(-s * j, 1 - layer), ref, at), (k_of(-s * j, layer), ref, height + at)]
    out += [(k_of(4, layer), far, at), (k_of(4, 1 - layer), sfar, at)]
    return out


def gather_xy(own, first, second):
    a, b = first(own, 1), first(own, -1)
    stack = jnp.concatenate([own, a, b, first(a, 1)], 0)
    half = stack.shape[0] // 2
    a, b = second(stack, 1), second(stack, -1)
    return [stack, a, b, second(a[:half], 1), second(b[half:], -1)]


def place_cols(dst, refs, y, x, y_first, height, at):
    for i, second in enumerate(RING4):
        for j, first in enumerate(RING4):
            if i < 3:
                ref, base = refs[i], j * height
            else:
                ref, base = refs[3 + j // 2], (j % 2) * height
            dy, dx = (first, second) if y_first else (second, first)
            k = lax.rem(y + dy + NY, NY) * NX + lax.rem(x + dx + NX, NX)
            dst[k, pl.ds(at, height), :] = ref[pl.ds(base, height), :]


def where_am_i():
    row = lax.axis_index("row")
    return row // NX, lax.rem(row, NX), lax.axis_index("col"), lax.axis_index("layer")


def mask_kernel(pos, pattern, density, cotangent, xg, mask):
    y, x, z, layer = pos[0], pos[1], pos[2], pos[3]
    r0 = (y * NX + x) * 2
    c0 = (z * 2 + layer) * 2
    rows, cols = pattern[0:1, :], pattern[1:2, :]
    for i in range(2):
        for j in range(2):
            hit = (rows == r0 + i) & (cols == c0 + j)
            on = jnp.max(jnp.where(hit, 1.0, 0.0).astype(F32), axis=1, keepdims=True)
            m = jnp.broadcast_to(on, (BS, BS)) > 0.5
            rs, cs = pl.ds(i * BS, BS), pl.ds(j * BS, BS)
            zero = jnp.zeros((BS, BS), F32)
            xg[rs, cs] = jnp.where(m, density[rs, cs].astype(F32), zero).astype(BF16)
            xg[pl.ds(T + i * BS, BS), cs] = jnp.where(m, cotangent[rs, cs].astype(F32), zero).astype(BF16)
            mask[rs, cs] = jnp.where(m, 1.0, 0.0).astype(F32)


def first_kernel(pos, mask, *refs):
    rows, cols, (sp, xc) = refs[:10], refs[10:15], refs[15:]
    y, x, z, layer = pos[0], pos[1], pos[2], pos[3]
    place_cols(xc, cols, y, x, True, T, 0)
    acc = jnp.zeros((2 * T, T), F32)
    for k, ref, at in row_pieces(rows, z, layer, 2 * T, 0, 2 * T):
        acc = acc + jnp.dot(ref[pl.ds(at, 2 * T), :], xc[k], preferred_element_type=F32)
    on = mask[...] > 0.5
    grad = rows[0][pl.ds(T, T), :].astype(F32)
    sp[pl.ds(0, T), :] = jnp.where(on, acc[:T], 0.0).astype(BF16)
    sp[pl.ds(T, T), :] = jnp.where(on, 3.0 * grad - 2.0 * acc[T:], 0.0).astype(BF16)


def second_kernel(pos, mask, *refs):
    xg_rows, sp_rows = refs[:10], refs[10:20]
    x_cols, g_cols, p_top, p_bot = refs[20:25], refs[25:30], refs[30:35], refs[35:40]
    out, xc, gc, pc = refs[40:]
    y, x, z, layer = pos[0], pos[1], pos[2], pos[3]
    place_cols(xc, x_cols, y, x, True, T, 0)
    place_cols(gc, g_cols, y, x, False, T, 0)
    place_cols(pc, p_top, y, x, True, BS, 0)
    place_cols(pc, p_bot, y, x, False, BS, BS)
    square = jnp.zeros((T, T), F32)
    rest = jnp.zeros((T, T), F32)
    for k, ref, at in row_pieces(sp_rows, z, layer, 2 * T, 0, T):
        square = square + jnp.dot(ref[pl.ds(at, T), :], gc[k], preferred_element_type=F32)
    for k, ref, at in row_pieces(sp_rows, z, layer, 2 * T, T, T):
        rest = rest + jnp.dot(ref[pl.ds(at, T), :], xc[k], preferred_element_type=F32)
    for k, ref, at in row_pieces(xg_rows, z, layer, 2 * T, 0, T):
        rest = rest + jnp.dot(ref[pl.ds(at, T), :], pc[k], preferred_element_type=F32)
    out[...] = jnp.where(mask[...] > 0.5, rest - 2.0 * square, 0.0)


def call(kernel, pos, args, out_shape, scratch=()):
    single = not isinstance(out_shape, (list, tuple))
    return pl.pallas_call(
        kernel,
        out_shape=out_shape,
        in_specs=[pl.BlockSpec(memory_space=pltpu.SMEM)] + [VMEM] * len(args),
        out_specs=VMEM if single else [VMEM] * len(out_shape),
        scratch_shapes=list(scratch),
        name=kernel.__name__,
    )(pos, *args)


def per_device(density, cotangent, block_pattern):
    pos = jnp.stack(where_am_i()).astype(jnp.int32)
    struct = jax.ShapeDtypeStruct
    xg, mask = call(
        mask_kernel, pos, (block_pattern, density, cotangent), [struct((2 * T, T), BF16), struct((T, T), F32)]
    )
    cols = pltpu.VMEM((NK, T, T), BF16)
    x_cols = gather_xy(xg[:T], shift_y, shift_x)
    g_cols = gather_xy(xg[T:], shift_x, shift_y)
    xg_rows = gather_z(xg)
    sp = call(first_kernel, pos, (mask, *xg_rows, *x_cols), struct((2 * T, T), BF16), [cols])
    p_top = gather_xy(sp[T : T + BS], shift_y, shift_x)
    p_bot = gather_xy(sp[T + BS :], shift_x, shift_y)
    sp_rows = gather_z(sp)
    return call(
        second_kernel,
        pos,
        (mask, *xg_rows, *sp_rows, *x_cols, *g_cols, *p_top, *p_bot),
        struct((T, T), F32),
        [cols, cols, cols],
    )


def solution(mesh):
    in_specs = (P("row", ("col", "layer")), P("row", ("col", "layer")), P())
    out_specs = P("row", ("col", "layer"))
    return jax.shard_map(
        per_device, mesh=mesh, in_specs=in_specs, out_specs=out_specs, check_vma=False
    )
```

```python
import jax
import jax.numpy as jnp
from jax import lax
from jax.experimental import pallas as pl
from jax.experimental.pallas import tpu as pltpu
from jax.sharding import PartitionSpec as P

BS = 128
T = 256
NX = NY = 4
NZ = 8
HALF = 2048
RING4 = (0, -1, 1, -2)


VMEM = pl.BlockSpec(memory_space=pltpu.VMEM)
SMEM = pl.BlockSpec(memory_space=pltpu.SMEM)
BF16 = jnp.bfloat16
F32 = jnp.float32


def shift_x(value, by):
    perm = [(y * NX + x, y * NX + (x + by) % NX) for y in range(NY) for x in range(NX)]
    return lax.ppermute(value, "row", perm)


def shift_y(value, by):
    perm = [(y * NX + x, ((y + by) % NY) * NX + x) for y in range(NY) for x in range(NX)]
    return lax.ppermute(value, "row", perm)


def shift_z(value, by):
    return lax.ppermute(value, "col", [(z, (z + by) % NZ) for z in range(NZ)])


def swap(value):
    return lax.ppermute(value, "layer", [(0, 1), (1, 0)])


def gather_z(own):
    out = [own]
    up = down = own
    for _ in range(3):
        up, down = shift_z(up, 1), shift_z(down, -1)
        out += [up, down]
    return [*out, shift_z(up[:T], 1), shift_z(down[T:], -1)]


def gather_xy(own, first, second):
    a, b = first(own, 1), first(own, -1)
    stack = jnp.concatenate([own, a, b, first(a, 1)], 0)
    half = stack.shape[0] // 2
    a, b = second(stack, 1), second(stack, -1)
    return [stack, a, b, second(a[:half], 1), second(b[half:], -1)]


def place_rows(refs, z, copies):
    for ref, dz in zip(refs[:7], (0, -1, 1, -2, 2, -3, 3)):
        at = pl.ds(pl.multiple_of(lax.rem(z + dz + NZ, NZ) * T, T), T)
        for dst, row in copies:
            dst[:, at] = ref[pl.ds(row, T), :]
    at = pl.ds(pl.multiple_of(lax.rem(z + 4, NZ) * T, T), T)
    for dst, row in copies:
        dst[:, at] = refs[7 + row // T][...]


def place_cols(dst, refs, y, x, y_first):
    for i, second in enumerate(RING4):
        for j, first in enumerate(RING4):
            ref, base = (refs[i], j * BS) if i < 3 else (refs[3 + j // 2], (j % 2) * BS)
            dy, dx = (first, second) if y_first else (second, first)
            k = lax.rem(y + dy + NY, NY) * NX + lax.rem(x + dx + NX, NX)
            dst[pl.ds(pl.multiple_of(k * BS, BS), BS), :] = ref[pl.ds(base, BS), :]


def start_kernel(pos, pattern, density, cotangent, density_sib, cotangent_sib, rows, x_col, g_col, flags):
    y, x, z, layer = pos[0], pos[1], pos[2], pos[3]
    r0, c0 = (y * NX + x) * 2, z * 4
    pr, pc = pattern[0:1, :], pattern[1:2, :]
    for i in range(2):
        for j in range(4):
            hit = (pr == r0 + i) & (pc == c0 + j)
            on = jnp.max(jnp.where(hit, 1.0, 0.0).astype(F32), axis=1, keepdims=True)
            flags[pl.ds(i * 4 + j, 1), :] = jnp.broadcast_to(on, (1, BS))
    zero = jnp.zeros((BS, BS), BF16)

    def fill(tile, d, g):
        half = pl.ds(pl.multiple_of(layer * BS, BS), BS)
        here = pl.ds(pl.multiple_of(tile * BS, BS), BS)
        for i in range(2):
            m = jnp.broadcast_to(flags[pl.ds(i * 4 + 2 * tile + layer, 1), :], (BS, BS)) > 0.5
            rs = pl.ds(i * BS, BS)
            rows[rs, here] = jnp.where(m, d[rs, half], zero)
            rows[pl.ds(T + i * BS, BS), here] = jnp.where(m, g[rs, half], zero)
            m = jnp.broadcast_to(flags[pl.ds(layer * 4 + 2 * tile + i, 1), :], (BS, BS)) > 0.5
            there = pl.ds(pl.multiple_of(tile * T + i * BS, BS), BS)
            x_col[:, there] = jnp.where(m, d[half, rs], zero)
            g_col[:, there] = jnp.where(m, g[half, rs], zero)

    fill(layer, density, cotangent)
    fill(1 - layer, density_sib, cotangent_sib)


def first_kernel(pos, *refs):
    rows, cols, (keep, send), (left_x, left_g, right, acc) = refs[:9], refs[9:14], refs[14:16], refs[16:]
    y, x, z, layer = pos[0], pos[1], pos[2], pos[3]
    place_cols(right, cols, y, x, True)
    place_rows(rows, z, [(left_x, 0), (left_g, T)])
    for n, left in enumerate((left_x, left_g)):
        acc[pl.ds(n * T, T), :] = jnp.dot(left[...], right[...], preferred_element_type=F32)
    for dst, h in ((keep, layer), (send, 1 - layer)):
        row = pl.ds(pl.multiple_of(T + h * BS, BS), BS)
        for t in range(2):
            here = pl.ds(t * BS, BS)
            dst[pl.ds(0, 2 * T), here] = acc[:, pl.ds(pl.multiple_of(t * T + h * BS, BS), BS)]
            dst[pl.ds(2 * T, BS), here] = acc[row, pl.ds(pl.multiple_of(t * T + (1 - h) * BS, BS), BS)]


def middle_kernel(pos, keep, got, rows, g_col, flags, sp_rows, p_col):
    layer = pos[3]

    def on(i, j):
        return jnp.broadcast_to(flags[pl.ds(i * 4 + j, 1), :], (BS, BS)) > 0.5

    def pulled(total, grad, m):
        return jnp.where(m, 3.0 * grad.astype(F32) - 2.0 * total, 0.0).astype(BF16)

    for t in range(2):
        here = pl.ds(t * BS, BS)
        for i in range(2):
            m = on(i, 2 * t + layer)
            at, pat = pl.ds(i * BS, BS), pl.ds(T + i * BS, BS)
            sp_rows[at, here] = jnp.where(m, keep[at, here] + got[at, here], 0.0).astype(BF16)
            sp_rows[pat, here] = pulled(keep[pat, here] + got[pat, here], rows[pat, here], m)
        mine = pl.ds(pl.multiple_of(t * T + layer * BS, BS), BS)
        p_col[:, mine] = sp_rows[pl.ds(pl.multiple_of(T + layer * BS, BS), BS), here]
        at = pl.ds(2 * T, BS)
        rest = pl.ds(pl.multiple_of(t * T + (1 - layer) * BS, BS), BS)
        p_col[:, rest] = pulled(keep[at, here] + got[at, here], g_col[:, rest], on(layer, 2 * t + 1 - layer))


def last_kernel(pos, *refs):
    rows, sp_rows, x_cols, g_cols, p_cols = refs[:9], refs[9:18], refs[18:23], refs[23:28], refs[28:33]
    flags, keep, send, left_x, left_s, left_p, right_x, right_g, right_p, acc = refs[33:]
    y, x, z, layer = pos[0], pos[1], pos[2], pos[3]
    place_cols(right_x, x_cols, y, x, True)
    place_cols(right_g, g_cols, y, x, False)
    place_cols(right_p, p_cols, y, x, True)
    place_rows(rows, z, [(left_x, 0)])
    place_rows(sp_rows, z, [(left_s, 0), (left_p, T)])
    total = -2.0 * jnp.dot(left_s[...], right_g[...], preferred_element_type=F32)
    total = total + jnp.dot(left_p[...], right_x[...], preferred_element_type=F32)
    acc[...] = total + jnp.dot(left_x[...], right_p[...], preferred_element_type=F32)
    for dst, t in ((keep, layer), (send, 1 - layer)):
        for i in range(2):
            for j in range(2):
                m = jnp.broadcast_to(flags[pl.ds(i * 4 + 2 * t + j, 1), :], (BS, BS)) > 0.5
                rs = pl.ds(i * BS, BS)
                block = acc[rs, pl.ds(pl.multiple_of(t * T + j * BS, BS), BS)]
                dst[rs, pl.ds(j * BS, BS)] = jnp.where(m, block, 0.0)


def call(kernel, pos, args, outs, scratch=()):
    return pl.pallas_call(
        kernel,
        out_shape=[jax.ShapeDtypeStruct(*o) for o in outs],
        in_specs=[SMEM] + [VMEM] * len(args),
        out_specs=[VMEM] * len(outs),
        scratch_shapes=[pltpu.VMEM(*s) for s in scratch],
        name=kernel.__name__,
    )(pos, *args)


def per_device(density, cotangent, block_pattern):
    row = lax.axis_index("row")
    pos = jnp.stack([row // NX, lax.rem(row, NX), lax.axis_index("col"), lax.axis_index("layer")])
    pos = pos.astype(jnp.int32)
    left, right = ((T, HALF), BF16), ((HALF, 2 * T), BF16)
    tall, wide = ((2 * T, T), BF16), ((BS, 2 * T), BF16)
    partial, tile = ((2 * T + BS, T), F32), ((T, T), F32)

    rows, x_col, g_col, flags = call(
        start_kernel,
        pos,
        (block_pattern, density, cotangent, swap(density), swap(cotangent)),
        [tall, wide, wide, ((8, BS), F32)],
    )
    x_cols = gather_xy(x_col, shift_y, shift_x)
    all_rows = gather_z(rows)
    g_cols = gather_xy(g_col, shift_x, shift_y)
    keep, send = call(
        first_kernel, pos, (*all_rows, *x_cols), [partial, partial], [left, left, right, ((2 * T, 2 * T), F32)]
    )
    sp, p_col = call(middle_kernel, pos, (keep, swap(send), rows, g_col, flags), [tall, wide])
    p_cols = gather_xy(p_col, shift_y, shift_x)
    sp_rows = gather_z(sp)
    keep, send = call(
        last_kernel,
        pos,
        (*all_rows, *sp_rows, *x_cols, *g_cols, *p_cols, flags),
        [tile, tile],
        [left] * 3 + [right] * 3 + [((T, 2 * T), F32)],
    )
    return keep + swap(send)


def solution(mesh):
    in_specs = (P("row", ("col", "layer")), P("row", ("col", "layer")), P())
    out_specs = P("row", ("col", "layer"))
    return jax.shard_map(
        per_device, mesh=mesh, in_specs=in_specs, out_specs=out_specs, check_vma=False
    )
```

```python
import jax
import jax.numpy as jnp
from jax import lax
from jax.experimental import pallas as pl
from jax.experimental.pallas import tpu as pltpu
from jax.sharding import PartitionSpec as P


BS = 128
T = 256
NX = NY = 4
NZ = 8
HALF = 2048
BULK = HALF - T
RING4 = (0, -1, 1, -2)


VMEM = pl.BlockSpec(memory_space=pltpu.VMEM)
SMEM = pl.BlockSpec(memory_space=pltpu.SMEM)
BF16 = jnp.bfloat16
F32 = jnp.float32


def shift_xy(value, by, y_core):
    perm = []
    for y in range(NY):
        for x in range(NX):
            for core in range(2):
                to = ((y + by) % NY) * NX + x if core == y_core else y * NX + (x + by) % NX
                perm.append(((y * NX + x) * 2 + core, to * 2 + core))
    return lax.ppermute(value, ("row", "layer"), perm)


def shift_z(value, by):
    return lax.ppermute(value, "col", [(z, (z + by) % NZ) for z in range(NZ)])


def swap(value):
    return lax.ppermute(value, "layer", [(0, 1), (1, 0)])


def gather_z(own):
    out = [own]
    up = down = own
    for _ in range(1, 4):
        up, down = shift_z(up, 1), shift_z(down, -1)
        out += [up, down]
    return [*out, shift_z(up[:T], 1), shift_z(down[T:], -1)]


def gather_xy(own):
    line = [own] + [shift_xy(own, by, 0) for by in (1, -1, 2)]
    stack = jnp.concatenate(line, 0)
    return [stack] + [shift_xy(stack, by, 1) for by in (1, -1, 2)]


def place_rows(refs, copies):
    for ref, dz in zip(refs[:7], (0, -1, 1, -2, 2, -3, 3)):
        for dst, row in copies:
            dst[:, pl.ds((dz + 3) * T, T)] = ref[pl.ds(row, T), :]


def place_cols(dst, refs, pos):
    y, x, z, layer = pos[0], pos[1], pos[2], pos[3]
    for i, second in enumerate(RING4):
        for j, first in enumerate(RING4):
            dy, dx = jnp.where(layer == 0, first, second), jnp.where(layer == 0, second, first)
            k = lax.rem(y + dy + NY, NY) * NX + lax.rem(x + dx + NX, NX)
            at = lax.rem(k // 2 - z + 3 + NZ, NZ) * T + lax.rem(k, 2) * BS
            dst[pl.ds(pl.multiple_of(at, BS), BS), :] = refs[i][pl.ds(j * BS, BS), :]


def dot(a, b):
    return jnp.dot(a, b, preferred_element_type=F32)


def load_kernel(pos, pattern, density, cotangent, flags, density_here, cotangent_here):
    y, x, z = pos[0], pos[1], pos[2]
    r0, c0 = (y * NX + x) * 2, z * 4
    pr, pc = pattern[0:1, :], pattern[1:2, :]
    for i in range(2):
        for j in range(4):
            hit = (pr == r0 + i) & (pc == c0 + j)
            on = jnp.max(jnp.where(hit, 1.0, 0.0).astype(F32), axis=1, keepdims=True)
            flags[pl.ds(i * 4 + j, 1), :] = jnp.broadcast_to(on, (1, BS))
    density_here[...] = density[...]
    cotangent_here[...] = cotangent[...]


def start_kernel(pos, flags, density, cotangent, density_sib, cotangent_sib, rows, x_col, g_col):
    layer = pos[3]
    zero = jnp.zeros((BS, BS), BF16)

    def fill(tile, d, g):
        half = pl.ds(pl.multiple_of(layer * BS, BS), BS)
        here = pl.ds(pl.multiple_of(tile * BS, BS), BS)
        for i in range(2):
            m = jnp.broadcast_to(flags[pl.ds(i * 4 + 2 * tile + layer, 1), :], (BS, BS)) > 0.5
            rs = pl.ds(i * BS, BS)
            rows[rs, here] = jnp.where(m, d[rs, half], zero)
            rows[pl.ds(T + i * BS, BS), here] = jnp.where(m, g[rs, half], zero)
            m = jnp.broadcast_to(flags[pl.ds(layer * 4 + 2 * tile + i, 1), :], (BS, BS)) > 0.5
            there = pl.ds(pl.multiple_of(tile * T + i * BS, BS), BS)
            x_col[:, there] = jnp.where(m, d[half, rs], zero)
            g_col[:, there] = jnp.where(m, g[half, rs], zero)

    fill(layer, density, cotangent)
    fill(1 - layer, density_sib, cotangent_sib)


def first_bulk(pos, *refs):
    rows, cols, (acc, right), (left_x, left_g) = refs[:7], refs[7:11], refs[11:13], refs[13:]
    place_cols(right, cols, pos)
    place_rows(rows, [(left_x, 0), (left_g, T)])
    for n, left in enumerate((left_x, left_g)):
        acc[pl.ds(n * T, T), :] = dot(left[...], right[pl.ds(0, BULK), :])


def first_rest(pos, bulk, right, x_last, g_last, keep, send, acc):
    layer = pos[3]
    for n, left in enumerate((x_last, g_last)):
        rs = pl.ds(n * T, T)
        acc[rs, :] = bulk[rs, :] + dot(left[...], right[pl.ds(BULK, T), :])
    for dst, h in ((keep, layer), (send, 1 - layer)):
        row = pl.ds(pl.multiple_of(T + h * BS, BS), BS)
        for t in range(2):
            here = pl.ds(t * BS, BS)
            dst[pl.ds(0, 2 * T), here] = acc[:, pl.ds(pl.multiple_of(t * T + h * BS, BS), BS)]
            dst[pl.ds(2 * T, BS), here] = acc[row, pl.ds(pl.multiple_of(t * T + (1 - h) * BS, BS), BS)]


def middle_kernel(pos, keep, got, rows, g_col, flags, sp_rows, p_col):
    layer = pos[3]

    def on(i, j):
        return jnp.broadcast_to(flags[pl.ds(i * 4 + j, 1), :], (BS, BS)) > 0.5

    def pulled(total, grad, m):
        return jnp.where(m, 3.0 * grad.astype(F32) - 2.0 * total, 0.0).astype(BF16)

    for t in range(2):
        here = pl.ds(t * BS, BS)
        for i in range(2):
            m = on(i, 2 * t + layer)
            at, pat = pl.ds(i * BS, BS), pl.ds(T + i * BS, BS)
            sp_rows[at, here] = jnp.where(m, keep[at, here] + got[at, here], 0.0).astype(BF16)
            sp_rows[pat, here] = pulled(keep[pat, here] + got[pat, here], rows[pat, here], m)
        mine = pl.ds(pl.multiple_of(t * T + layer * BS, BS), BS)
        p_col[:, mine] = sp_rows[pl.ds(pl.multiple_of(T + layer * BS, BS), BS), here]
        at = pl.ds(2 * T, BS)
        rest = pl.ds(pl.multiple_of(t * T + (1 - layer) * BS, BS), BS)
        p_col[:, rest] = pulled(keep[at, here] + got[at, here], g_col[:, rest], on(layer, 2 * t + 1 - layer))


def last_bulk(pos, *refs):
    rows, sp_rows, right_x, g_cols, p_cols = refs[:8], refs[8:15], refs[15], refs[16:20], refs[20:24]
    acc, g_last, left_x, left_s, left_p, right_g, right_p = refs[24:]
    place_cols(right_g, g_cols, pos)
    place_cols(right_p, p_cols, pos)
    place_rows(rows, [(left_x, 0)])
    left_x[:, pl.ds(BULK, T)] = rows[7][...]
    place_rows(sp_rows, [(left_s, 0), (left_p, T)])
    total = -2.0 * dot(left_s[...], right_g[pl.ds(0, BULK), :])
    total = total + dot(left_p[...], right_x[pl.ds(0, BULK), :])
    acc[...] = total + dot(left_x[...], right_p[...])
    g_last[...] = right_g[pl.ds(BULK, T), :]


def last_rest(pos, bulk, g_last, right_x, s_last, p_last, flags, keep, send, acc):
    layer = pos[3]
    total = bulk[...] - 2.0 * dot(s_last[...], g_last[...])
    acc[...] = total + dot(p_last[...], right_x[pl.ds(BULK, T), :])
    for dst, t in ((keep, layer), (send, 1 - layer)):
        for i in range(2):
            for j in range(2):
                m = jnp.broadcast_to(flags[pl.ds(i * 4 + 2 * t + j, 1), :], (BS, BS)) > 0.5
                rs = pl.ds(i * BS, BS)
                block = acc[rs, pl.ds(pl.multiple_of(t * T + j * BS, BS), BS)]
                dst[rs, pl.ds(j * BS, BS)] = jnp.where(m, block, 0.0)


def call(kernel, pos, args, outs, mib, scratch=()):
    return pl.pallas_call(
        kernel,
        out_shape=[jax.ShapeDtypeStruct(*o) for o in outs],
        in_specs=[SMEM] + [VMEM] * len(args),
        out_specs=[VMEM] * len(outs),
        scratch_shapes=[pltpu.VMEM(*s) for s in scratch],
        compiler_params=pltpu.CompilerParams(vmem_limit_bytes=mib << 20),
    )(pos, *args)


def step(density, cotangent, block_pattern):
    row = lax.axis_index("row")
    pos = jnp.stack([row // NX, lax.rem(row, NX), lax.axis_index("col"), lax.axis_index("layer")])
    pos = pos.astype(jnp.int32)
    left, right = ((T, BULK), BF16), ((HALF, 2 * T), BF16)
    tall, wide = ((2 * T, T), BF16), ((BS, 2 * T), BF16)
    partial, tile, own = ((2 * T + BS, T), F32), ((T, T), F32), ((T, T), BF16)

    density_sib, cotangent_sib = swap(density), swap(cotangent)
    flags, density, cotangent = call(
        load_kernel, pos, (block_pattern, density, cotangent), [((8, BS), F32), own, own], 4
    )
    rows, x_col, g_col = call(
        start_kernel, pos, (flags, density, cotangent, density_sib, cotangent_sib), [tall, wide, wide], 4
    )
    x_cols = gather_xy(x_col)
    all_rows = gather_z(rows)
    g_cols = gather_xy(g_col)
    bulk, right_x = call(
        first_bulk, pos, (*all_rows[:7], *x_cols), [((2 * T, 2 * T), F32), right], 16, [left, left]
    )
    keep, send = call(
        first_rest, pos, (bulk, right_x, *all_rows[7:]), [partial, partial], 12, [((2 * T, 2 * T), F32)]
    )
    sp, p_col = call(middle_kernel, pos, (keep, swap(send), rows, g_col, flags), [tall, wide], 6)
    p_cols = gather_xy(p_col)
    sp_rows = gather_z(sp)
    bulk, g_last = call(
        last_bulk,
        pos,
        (*all_rows[:8], *sp_rows[:7], right_x, *g_cols, *p_cols),
        [((T, 2 * T), F32), ((T, 2 * T), BF16)],
        28,
        [((T, HALF), BF16), left, left, right, right],
    )
    keep, send = call(
        last_rest, pos, (bulk, g_last, right_x, *sp_rows[7:], flags), [tile, tile], 8, [((T, 2 * T), F32)]
    )
    return keep + swap(send)


def solution(mesh):
    in_specs = (P("row", ("col", "layer")), P("row", ("col", "layer")), P())
    out_specs = P("row", ("col", "layer"))
    return jax.shard_map(step, mesh=mesh, in_specs=in_specs, out_specs=out_specs, check_vma=False)
```

```python
import jax
import jax.numpy as jnp
from jax import lax
from jax.experimental import pallas as pl
from jax.experimental.pallas import tpu as pltpu
from jax.sharding import PartitionSpec as P


BS = 128
T = 256
NX = NY = 4
NZ = 8
HALF = 2048
BULK = HALF - T
RING4 = (0, -1, 1, -2)


VMEM = pl.BlockSpec(memory_space=pltpu.VMEM)
SMEM = pl.BlockSpec(memory_space=pltpu.SMEM)
BF16 = jnp.bfloat16
F32 = jnp.float32


def shift_xy(value, by, y_core):
    perm = []
    for y in range(NY):
        for x in range(NX):
            for core in range(2):
                to = ((y + by) % NY) * NX + x if core == y_core else y * NX + (x + by) % NX
                perm.append(((y * NX + x) * 2 + core, to * 2 + core))
    return lax.ppermute(value, ("row", "layer"), perm)


def shift_z(value, by):
    return lax.ppermute(value, "col", [(z, (z + by) % NZ) for z in range(NZ)])


def swap(value):
    return lax.ppermute(value, "layer", [(0, 1), (1, 0)])


def gather_z(own):
    out = [own]
    up = down = own
    for _ in range(1, 4):
        up, down = shift_z(up, 1), shift_z(down, -1)
        out += [up, down]
    return [*out, shift_z(up[:T], 1), shift_z(down[T:], -1)]


def gather_xy(own):
    line = [own] + [shift_xy(own, by, 0) for by in (1, -1, 2)]
    stack = pl.pallas_call(
        stack_kernel,
        out_shape=jax.ShapeDtypeStruct((4 * BS, 2 * T), BF16),
        in_specs=[VMEM] * 4,
        out_specs=VMEM,
        compiler_params=pltpu.CompilerParams(vmem_limit_bytes=4 << 20),
    )(*line)
    return [stack] + [shift_xy(stack, by, 1) for by in (1, -1, 2)]


def place_rows(refs, copies):
    for ref, dz in zip(refs[:7], (0, -1, 1, -2, 2, -3, 3)):
        for dst, row in copies:
            dst[:, pl.ds((dz + 3) * T, T)] = ref[pl.ds(row, T), :]


def place_cols(dst, refs, pos):
    y, x, z, layer = pos[0], pos[1], pos[2], pos[3]
    for i, second in enumerate(RING4):
        for j, first in enumerate(RING4):
            dy, dx = jnp.where(layer == 0, first, second), jnp.where(layer == 0, second, first)
            k = lax.rem(y + dy + NY, NY) * NX + lax.rem(x + dx + NX, NX)
            at = lax.rem(k // 2 - z + 3 + NZ, NZ) * T + lax.rem(k, 2) * BS
            dst[pl.ds(pl.multiple_of(at, BS), BS), :] = refs[i][pl.ds(j * BS, BS), :]


def stack_kernel(*refs):
    for i, ref in enumerate(refs[:4]):
        refs[4][pl.ds(i * BS, BS), :] = ref[...]


def dot(a, b):
    return jnp.dot(a, b, preferred_element_type=F32)


def flags_kernel(pos, pattern, flags):
    y, x, z = pos[0], pos[1], pos[2]
    r0, c0 = (y * NX + x) * 2, z * 4
    pr, pc = pattern[0:1, :], pattern[1:2, :]
    for i in range(2):
        for j in range(4):
            hit = (pr == r0 + i) & (pc == c0 + j)
            on = jnp.max(jnp.where(hit, 1.0, 0.0).astype(F32), axis=1, keepdims=True)
            flags[pl.ds(i * 4 + j, 1), :] = jnp.broadcast_to(on, (1, BS))


def start_kernel(pos, flags, both, both_sib, rows, x_col, g_col):
    layer = pos[3]
    zero = jnp.zeros((BS, BS), BF16)

    def fill(tile, dg):
        lanes = pl.ds(pl.multiple_of(layer * BS, BS), BS)
        here = pl.ds(pl.multiple_of(tile * BS, BS), BS)
        for i in range(2):
            m = jnp.broadcast_to(flags[pl.ds(i * 4 + 2 * tile + layer, 1), :], (BS, BS)) > 0.5
            for n in range(2):
                rs = pl.ds(n * T + i * BS, BS)
                rows[rs, here] = jnp.where(m, dg[rs, lanes], zero)
            m = jnp.broadcast_to(flags[pl.ds(layer * 4 + 2 * tile + i, 1), :], (BS, BS)) > 0.5
            there = pl.ds(pl.multiple_of(tile * T + i * BS, BS), BS)
            for n, col in enumerate((x_col, g_col)):
                half = pl.ds(pl.multiple_of(n * T + layer * BS, BS), BS)
                col[:, there] = jnp.where(m, dg[half, pl.ds(i * BS, BS)], zero)

    fill(layer, both)
    fill(1 - layer, both_sib)


def first_bulk(pos, *refs):
    rows, cols, (acc, right), (left_x, left_g) = refs[:7], refs[7:11], refs[11:13], refs[13:]
    place_cols(right, cols, pos)
    place_rows(rows, [(left_x, 0), (left_g, T)])
    for n, left in enumerate((left_x, left_g)):
        acc[pl.ds(n * T, T), :] = dot(left[...], right[pl.ds(0, BULK), :])


def first_rest(pos, bulk, right, x_last, g_last, keep, send, acc):
    layer = pos[3]
    for n, left in enumerate((x_last, g_last)):
        rs = pl.ds(n * T, T)
        acc[rs, :] = bulk[rs, :] + dot(left[...], right[pl.ds(BULK, T), :])
    for dst, h in ((keep, layer), (send, 1 - layer)):
        row = pl.ds(pl.multiple_of(T + h * BS, BS), BS)
        for t in range(2):
            here = pl.ds(t * BS, BS)
            dst[pl.ds(0, 2 * T), here] = acc[:, pl.ds(pl.multiple_of(t * T + h * BS, BS), BS)]
            dst[pl.ds(2 * T, BS), here] = acc[row, pl.ds(pl.multiple_of(t * T + (1 - h) * BS, BS), BS)]


def middle_kernel(pos, keep, got, rows, g_col, flags, sp_rows, p_col):
    layer = pos[3]

    def on(i, j):
        return jnp.broadcast_to(flags[pl.ds(i * 4 + j, 1), :], (BS, BS)) > 0.5

    def pulled(total, grad, m):
        return jnp.where(m, 3.0 * grad.astype(F32) - 2.0 * total, 0.0).astype(BF16)

    for t in range(2):
        here = pl.ds(t * BS, BS)
        for i in range(2):
            m = on(i, 2 * t + layer)
            at, pat = pl.ds(i * BS, BS), pl.ds(T + i * BS, BS)
            sp_rows[at, here] = jnp.where(m, keep[at, here] + got[at, here], 0.0).astype(BF16)
            sp_rows[pat, here] = pulled(keep[pat, here] + got[pat, here], rows[pat, here], m)
        mine = pl.ds(pl.multiple_of(t * T + layer * BS, BS), BS)
        p_col[:, mine] = sp_rows[pl.ds(pl.multiple_of(T + layer * BS, BS), BS), here]
        at = pl.ds(2 * T, BS)
        rest = pl.ds(pl.multiple_of(t * T + (1 - layer) * BS, BS), BS)
        p_col[:, rest] = pulled(keep[at, here] + got[at, here], g_col[:, rest], on(layer, 2 * t + 1 - layer))


def last_bulk(pos, *refs):
    rows, sp_rows, right_x, g_cols, p_cols = refs[:8], refs[8:15], refs[15], refs[16:20], refs[20:24]
    acc, g_last, left_x, left_s, left_p, right_g, right_p = refs[24:]
    place_cols(right_g, g_cols, pos)
    place_cols(right_p, p_cols, pos)
    place_rows(rows, [(left_x, 0)])
    left_x[:, pl.ds(BULK, T)] = rows[7][...]
    place_rows(sp_rows, [(left_s, 0), (left_p, T)])
    total = -2.0 * dot(left_s[...], right_g[pl.ds(0, BULK), :])
    total = total + dot(left_p[...], right_x[pl.ds(0, BULK), :])
    acc[...] = total + dot(left_x[...], right_p[...])
    g_last[...] = right_g[pl.ds(BULK, T), :]


def last_rest(pos, bulk, g_last, right_x, s_last, p_last, flags, keep, send, acc):
    layer = pos[3]
    total = bulk[...] - 2.0 * dot(s_last[...], g_last[...])
    acc[...] = total + dot(p_last[...], right_x[pl.ds(BULK, T), :])
    for dst, t in ((keep, layer), (send, 1 - layer)):
        for i in range(2):
            for j in range(2):
                m = jnp.broadcast_to(flags[pl.ds(i * 4 + 2 * t + j, 1), :], (BS, BS)) > 0.5
                rs = pl.ds(i * BS, BS)
                block = acc[rs, pl.ds(pl.multiple_of(t * T + j * BS, BS), BS)]
                dst[rs, pl.ds(j * BS, BS)] = jnp.where(m, block, 0.0)


def call(kernel, pos, args, outs, mib, scratch=()):
    return pl.pallas_call(
        kernel,
        out_shape=[jax.ShapeDtypeStruct(*o) for o in outs],
        in_specs=[SMEM] + [VMEM] * len(args),
        out_specs=[VMEM] * len(outs),
        scratch_shapes=[pltpu.VMEM(*s) for s in scratch],
        compiler_params=pltpu.CompilerParams(vmem_limit_bytes=mib << 20),
    )(pos, *args)


def step(density, cotangent, block_pattern):
    row = lax.axis_index("row")
    pos = jnp.stack([row // NX, lax.rem(row, NX), lax.axis_index("col"), lax.axis_index("layer")])
    pos = pos.astype(jnp.int32)
    left, right = ((T, BULK), BF16), ((HALF, 2 * T), BF16)
    tall, wide = ((2 * T, T), BF16), ((BS, 2 * T), BF16)
    partial, tile = ((2 * T + BS, T), F32), ((T, T), F32)

    both = jnp.concatenate([density, cotangent], 0)
    both_sib = swap(both)
    (flags,) = call(flags_kernel, pos, (block_pattern,), [((8, BS), F32)], 2)
    rows, x_col, g_col = call(start_kernel, pos, (flags, both, both_sib), [tall, wide, wide], 4)
    x_cols = gather_xy(x_col)
    all_rows = gather_z(rows)
    g_cols = gather_xy(g_col)
    bulk, right_x = call(
        first_bulk, pos, (*all_rows[:7], *x_cols), [((2 * T, 2 * T), F32), right], 16, [left, left]
    )
    keep, send = call(
        first_rest, pos, (bulk, right_x, *all_rows[7:]), [partial, partial], 12, [((2 * T, 2 * T), F32)]
    )
    sp, p_col = call(middle_kernel, pos, (keep, swap(send), rows, g_col, flags), [tall, wide], 6)
    p_cols = gather_xy(p_col)
    sp_rows = gather_z(sp)
    bulk, g_last = call(
        last_bulk,
        pos,
        (*all_rows[:8], *sp_rows[:7], right_x, *g_cols, *p_cols),
        [((T, 2 * T), F32), ((T, 2 * T), BF16)],
        28,
        [((T, HALF), BF16), left, left, right, right],
    )
    keep, send = call(
        last_rest, pos, (bulk, g_last, right_x, *sp_rows[7:], flags), [tile, tile], 8, [((T, 2 * T), F32)]
    )
    return keep + swap(send)


def solution(mesh):
    in_specs = (P("row", ("col", "layer")), P("row", ("col", "layer")), P())
    out_specs = P("row", ("col", "layer"))
    return jax.shard_map(step, mesh=mesh, in_specs=in_specs, out_specs=out_specs, check_vma=False)
```

```python
import jax
import jax.numpy as jnp
from jax import lax
from jax.experimental import pallas as pl
from jax.experimental.pallas import tpu as pltpu
from jax.sharding import PartitionSpec as P


BS = 128
T = 256
NX = NY = 4
NZ = 8
HALF = 2048
BULK = HALF - T
RING4 = (0, -1, 1, -2)
RING8 = (0, -1, 1, -2, 2, -3, 3)


VMEM = pl.BlockSpec(memory_space=pltpu.VMEM)
SMEM = pl.BlockSpec(memory_space=pltpu.SMEM)
BF16 = jnp.bfloat16
F32 = jnp.float32


def shift_xy(value, by, y_core):
    perm = []
    for y in range(NY):
        for x in range(NX):
            for core in range(2):
                to = ((y + by) % NY) * NX + x if core == y_core else y * NX + (x + by) % NX
                perm.append(((y * NX + x) * 2 + core, to * 2 + core))
    return lax.ppermute(value, ("row", "layer"), perm)


def shift_z(value, by):
    perm = [(z * 2 + core, (z + (by, -by)[core]) % NZ * 2 + core) for z in range(NZ) for core in range(2)]
    return lax.ppermute(value, ("col", "layer"), perm)


def swap(value):
    return lax.ppermute(value, "layer", [(0, 1), (1, 0)])


def gather_z(own):
    out = [own]
    ahead = behind = own
    for _ in range(1, 4):
        ahead, behind = shift_z(ahead, 1), shift_z(behind, -1)
        out += [ahead, behind]
    return [*out, shift_z(ahead, 1)]


def gather_xy(own):
    line = [own] + [shift_xy(own, by, 0) for by in (1, -1, 2)]
    (stack,) = call(stack_kernel, None, line, [((4 * BS, 2 * T), BF16)], 4)
    return [stack] + [shift_xy(stack, by, 1) for by in (1, -1, 2)]


def place_rows(refs, copies, pos):
    for ref, dz in zip(refs[:7], RING8):
        at = (jnp.where(pos[3] == 0, dz, -dz) + 3) * T
        for dst, row in copies:
            dst[:, pl.ds(pl.multiple_of(at, T), T)] = ref[pl.ds(row, T), :]


def place_cols(dst, refs, pos):
    y, x, z, layer = pos[0], pos[1], pos[2], pos[3]
    for i, second in enumerate(RING4):
        for j, first in enumerate(RING4):
            dy, dx = jnp.where(layer == 0, first, second), jnp.where(layer == 0, second, first)
            k = lax.rem(y + dy + NY, NY) * NX + lax.rem(x + dx + NX, NX)
            at = lax.rem(k // 2 - z + 3 + NZ, NZ) * T + lax.rem(k, 2) * BS
            dst[pl.ds(pl.multiple_of(at, BS), BS), :] = refs[i][pl.ds(j * BS, BS), :]


def stack_kernel(*refs):
    for i, ref in enumerate(refs[:4]):
        refs[4][pl.ds(i * BS, BS), :] = ref[...]


def dot(a, b):
    return jnp.dot(a, b, preferred_element_type=F32)


def flags_kernel(pos, pattern, flags):
    y, x, z = pos[0], pos[1], pos[2]
    r0, c0 = (y * NX + x) * 2, z * 4
    pr, pc = pattern[0:1, :], pattern[1:2, :]
    for i in range(2):
        for j in range(4):
            hit = (pr == r0 + i) & (pc == c0 + j)
            on = jnp.max(jnp.where(hit, 1.0, 0.0).astype(F32), axis=1, keepdims=True)
            flags[pl.ds(i * 4 + j, 1), :] = jnp.broadcast_to(on, (1, BS))


def start_kernel(pos, flags, both, both_sib, rows, x_col, g_col):
    layer = pos[3]
    zero = jnp.zeros((BS, BS), BF16)

    def fill(tile, dg):
        lanes = pl.ds(pl.multiple_of(layer * BS, BS), BS)
        here = pl.ds(pl.multiple_of(tile * BS, BS), BS)
        for i in range(2):
            m = jnp.broadcast_to(flags[pl.ds(i * 4 + 2 * tile + layer, 1), :], (BS, BS)) > 0.5
            for n in range(2):
                rs = pl.ds(n * T + i * BS, BS)
                rows[rs, here] = jnp.where(m, dg[rs, lanes], zero)
            m = jnp.broadcast_to(flags[pl.ds(layer * 4 + 2 * tile + i, 1), :], (BS, BS)) > 0.5
            there = pl.ds(pl.multiple_of(tile * T + i * BS, BS), BS)
            for n, col in enumerate((x_col, g_col)):
                half = pl.ds(pl.multiple_of(n * T + layer * BS, BS), BS)
                col[:, there] = jnp.where(m, dg[half, pl.ds(i * BS, BS)], zero)

    fill(layer, both)
    fill(1 - layer, both_sib)


def first_bulk(pos, *refs):
    rows, cols, (acc, right), (left_x, left_g) = refs[:7], refs[7:11], refs[11:13], refs[13:]
    place_cols(right, cols, pos)
    place_rows(rows, [(left_x, 0), (left_g, T)], pos)
    for n, left in enumerate((left_x, left_g)):
        acc[pl.ds(n * T, T), :] = dot(left[...], right[pl.ds(0, BULK), :])


def first_rest(pos, bulk, right, last, keep, send, acc):
    layer = pos[3]
    for n in range(2):
        rs = pl.ds(n * T, T)
        acc[rs, :] = bulk[rs, :] + dot(last[rs, :], right[pl.ds(BULK, T), :])
    for dst, h in ((keep, layer), (send, 1 - layer)):
        row = pl.ds(pl.multiple_of(T + h * BS, BS), BS)
        for t in range(2):
            here = pl.ds(t * BS, BS)
            dst[pl.ds(0, 2 * T), here] = acc[:, pl.ds(pl.multiple_of(t * T + h * BS, BS), BS)]
            dst[pl.ds(2 * T, BS), here] = acc[row, pl.ds(pl.multiple_of(t * T + (1 - h) * BS, BS), BS)]


def middle_kernel(pos, keep, got, rows, g_col, flags, sp_rows, p_col):
    layer = pos[3]

    def on(i, j):
        return jnp.broadcast_to(flags[pl.ds(i * 4 + j, 1), :], (BS, BS)) > 0.5

    def pulled(total, grad, m):
        return jnp.where(m, 3.0 * grad.astype(F32) - 2.0 * total, 0.0).astype(BF16)

    for t in range(2):
        here = pl.ds(t * BS, BS)
        for i in range(2):
            m = on(i, 2 * t + layer)
            at, pat = pl.ds(i * BS, BS), pl.ds(T + i * BS, BS)
            sp_rows[at, here] = jnp.where(m, keep[at, here] + got[at, here], 0.0).astype(BF16)
            sp_rows[pat, here] = pulled(keep[pat, here] + got[pat, here], rows[pat, here], m)
        mine = pl.ds(pl.multiple_of(t * T + layer * BS, BS), BS)
        p_col[:, mine] = sp_rows[pl.ds(pl.multiple_of(T + layer * BS, BS), BS), here]
        at = pl.ds(2 * T, BS)
        rest = pl.ds(pl.multiple_of(t * T + (1 - layer) * BS, BS), BS)
        p_col[:, rest] = pulled(keep[at, here] + got[at, here], g_col[:, rest], on(layer, 2 * t + 1 - layer))


def last_bulk(pos, *refs):
    rows, sp_rows, right_x, g_cols, p_cols = refs[:8], refs[8:15], refs[15], refs[16:20], refs[20:24]
    acc, g_last, left_x, left_s, left_p, right_g, right_p = refs[24:]
    place_cols(right_g, g_cols, pos)
    place_cols(right_p, p_cols, pos)
    place_rows(rows, [(left_x, 0)], pos)
    left_x[:, pl.ds(BULK, T)] = rows[7][pl.ds(0, T), :]
    place_rows(sp_rows, [(left_s, 0), (left_p, T)], pos)
    total = -2.0 * dot(left_s[...], right_g[pl.ds(0, BULK), :])
    total = total + dot(left_p[...], right_x[pl.ds(0, BULK), :])
    acc[...] = total + dot(left_x[...], right_p[...])
    g_last[...] = right_g[pl.ds(BULK, T), :]


def last_rest(pos, bulk, g_last, right_x, last, flags, keep, send, acc):
    layer = pos[3]
    total = bulk[...] - 2.0 * dot(last[pl.ds(0, T), :], g_last[...])
    acc[...] = total + dot(last[pl.ds(T, T), :], right_x[pl.ds(BULK, T), :])
    for dst, t in ((keep, layer), (send, 1 - layer)):
        for i in range(2):
            for j in range(2):
                m = jnp.broadcast_to(flags[pl.ds(i * 4 + 2 * t + j, 1), :], (BS, BS)) > 0.5
                rs = pl.ds(i * BS, BS)
                block = acc[rs, pl.ds(pl.multiple_of(t * T + j * BS, BS), BS)]
                dst[rs, pl.ds(j * BS, BS)] = jnp.where(m, block, 0.0)


def call(kernel, pos, args, outs, mib, scratch=()):
    return pl.pallas_call(
        kernel,
        out_shape=[jax.ShapeDtypeStruct(*o) for o in outs],
        in_specs=[SMEM] * (pos is not None) + [VMEM] * len(args),
        out_specs=[VMEM] * len(outs),
        scratch_shapes=[pltpu.VMEM(*s) for s in scratch],
        compiler_params=pltpu.CompilerParams(vmem_limit_bytes=mib << 20),
    )(*([] if pos is None else [pos]), *args)


def step(density, cotangent, block_pattern):
    row = lax.axis_index("row")
    pos = jnp.stack([row // NX, lax.rem(row, NX), lax.axis_index("col"), lax.axis_index("layer")])
    pos = pos.astype(jnp.int32)
    left, right = ((T, BULK), BF16), ((HALF, 2 * T), BF16)
    tall, wide = ((2 * T, T), BF16), ((BS, 2 * T), BF16)
    partial, tile = ((2 * T + BS, T), F32), ((T, T), F32)

    low = jnp.array(-jnp.inf, BF16)
    below, above = ((0, T, 0), (0, 0, 0)), ((T, 0, 0), (0, 0, 0))
    both = jnp.maximum(lax.pad(density, low, below), lax.pad(cotangent, low, above))
    both_sib = swap(both)
    (flags,) = call(flags_kernel, pos, (block_pattern,), [((8, BS), F32)], 2)
    rows, x_col, g_col = call(start_kernel, pos, (flags, both, both_sib), [tall, wide, wide], 4)
    all_rows = gather_z(rows)
    x_cols, g_cols = gather_xy(x_col), gather_xy(g_col)
    bulk, right_x = call(
        first_bulk, pos, (*all_rows[:7], *x_cols), [((2 * T, 2 * T), F32), right], 16, [left, left]
    )
    keep, send = call(
        first_rest, pos, (bulk, right_x, *all_rows[7:]), [partial, partial], 12, [((2 * T, 2 * T), F32)]
    )
    got = swap(send)
    sp, p_col = call(middle_kernel, pos, (keep, got, rows, g_col, flags), [tall, wide], 6)
    p_cols = gather_xy(p_col)
    sp_rows = gather_z(sp)
    bulk, g_last = call(
        last_bulk,
        pos,
        (*all_rows[:8], *sp_rows[:7], right_x, *g_cols, *p_cols),
        [((T, 2 * T), F32), ((T, 2 * T), BF16)],
        28,
        [((T, HALF), BF16), left, left, right, right],
    )
    keep, send = call(
        last_rest, pos, (bulk, g_last, right_x, *sp_rows[7:], flags), [tile, tile], 8, [((T, 2 * T), F32)]
    )
    return keep + swap(send)


def solution(mesh):
    in_specs = (P("row", ("col", "layer")), P("row", ("col", "layer")), P())
    out_specs = P("row", ("col", "layer"))
    return jax.shard_map(step, mesh=mesh, in_specs=in_specs, out_specs=out_specs, check_vma=False)
```
